32 devices in a mesh: dp: 8 (over z, x), tensor: 4 (over y, core).
Axes of the slice: x: 2, y: 2, z: 4, core: 2. Of those that a mesh axis runs over, the one named last changes fastest.
Arguments:
- tokens: bfloat16 [512, 4096], P('dp', 'tensor')
- norm_gain: float32 [4096], P('tensor'), may hold values from 0.5 to 1.5
- eraser_mean: float32 [4096], P('tensor'), may hold values from -6 to 6
- eraser_in: float32 [4096, 128], P('tensor'), may hold values from -0.09375 to 0.09375
- eraser_out: float32 [4096, 128], P('tensor'), may hold values from -0.5 to 0.5
- router: float32 [4096, 8], P('tensor'), may hold values from -0.09375 to 0.09375
- expert_ids: int32 [512, 2], P('dp'), may hold values from 0 to 7, as said below
- slots: int32 [512, 2], P('dp'), may hold values from 0 to 63, as said below
- w_gate: bfloat16 [8, 4096, 14336], P('dp', None, 'tensor'), may hold values from -0.09375 to 0.09375
- w_up: bfloat16 [8, 4096, 14336], P('dp', None, 'tensor'), may hold values from -0.09375 to 0.09375
- w_down: bfloat16 [8, 14336, 4096], P('dp', 'tensor'), may hold values from -0.0625 to 0.0625
Outputs:
- moe_out: bfloat16 [512, 4096], P('dp', 'tensor')
The draws below stay inside these ranges and needn't reach their ends.
Inputs may be any that keep to these rules, and one draw needn't show every extreme that they name: `expert_ids`: the two experts of a token differ. Within each aligned block of 64 tokens, the choices naming one expert have the slots 0, 1, 2, ... with no repeats; choices with a slot of 24 or more are dropped.
All inputs are finite; a program needn't handle non-finite values.
Results may differ from the reference program's by a relative error of at most 0.0065.
Values may be sent and summed in bfloat16 or wider, within the bound.
A program may use at most 128 MiB of HBM per device.

```python
import jax
import jax.numpy as jnp
from jax import lax

D = 4096
FF = 14336
E = 8
K = 128
TOK_DEV = 64
CAP = 24
FF_PARTS = 1
TOKENS = 512


def route_table(key):
    folded = jax.random.fold_in(key, 11)
    key_hot, key_bias, key_jitter, key_order = jax.random.split(folded, 4)
    expert_range = jnp.arange(E, dtype=jnp.int32)
    hot_expert = jax.random.randint(key_hot, (), 0, E, dtype=jnp.int32)
    expert_bias = jax.random.randint(key_bias, (E,), 0, 24, dtype=jnp.int32) + 200 * (expert_range == hot_expert).astype(jnp.int32)
    jitter = jax.random.randint(key_jitter, (TOKENS, E), 0, 64, dtype=jnp.int32)
    scores = (jitter + expert_bias[None, :]) * E + expert_range[None, :]
    unused, chosen = lax.top_k(scores, 2)
    chosen = chosen.astype(jnp.int32)
    priority = jax.random.randint(key_order, (TOKENS,), 0, 4096, dtype=jnp.int32) * TOKENS + jnp.arange(TOKENS, dtype=jnp.int32)
    blocks = TOKENS // TOK_DEV
    onehot = jnp.sum((chosen[:, :, None] == expert_range[None, None, :]).astype(jnp.int32), axis=1).reshape(blocks, TOK_DEV, E)
    ordered = priority.reshape(blocks, TOK_DEV)
    earlier = (ordered[:, None, :] < ordered[:, :, None]).astype(jnp.int32)
    ranks = jnp.sum(earlier[:, :, :, None] * onehot[:, None, :, :], axis=2).reshape(TOKENS, E)
    slot_table = jnp.take_along_axis(ranks, chosen, axis=1).astype(jnp.int32)
    return (chosen, slot_table)


def draw_expert_ids(key, part):
    return route_table(key)[0]


def draw_slots(key, part):
    return route_table(key)[1]


def draw_tokens(key, part):
    key_rows, key_cols, key_base = jax.random.split(jax.random.fold_in(key, 5), 3)
    col_scale = 3.0 ** (jnp.arange(D, dtype=jnp.float32) / D) * jnp.exp(jax.random.uniform(key_cols, (1, D), jnp.float32, -0.5, 0.5))
    row_scale = jnp.exp(jax.random.uniform(key_rows, (TOKENS, 1), jnp.float32) * jnp.log(10.0))
    base = jnp.clip(jax.random.normal(key_base, (TOKENS, D), jnp.float32), -5.0, 5.0)
    return (base * row_scale * col_scale).astype(jnp.bfloat16)


def spiked(drawn, stream_key, source, target, shards_of, factor):
    owner, partner = [(jnp.arange(drawn.shape[dim]) // (drawn.shape[dim] // shards_of)).reshape([-1 if axis == dim else 1 for axis in range(drawn.ndim)]) for dim in (source, target)]
    chosen = jax.random.permutation(stream_key, shards_of)[partner]
    strong = (owner == chosen) | (owner == (partner + shards_of // 2) % shards_of)
    return jnp.where(strong, factor * drawn, drawn)


def steps_of(rng, extent, shards, smallest, top_value):
    def one(dim, shards_of):
        heights = jax.random.uniform(jax.random.fold_in(jax.random.fold_in(rng, 6), dim), (shards_of,), jnp.float32, smallest / len(shards), top_value / len(shards))
        return jnp.repeat(jnp.exp(heights), extent[dim] // shards_of).reshape((-1,) + (1,) * (len(extent) - dim - 1))

    gain = one(*shards[0])
    for cut in shards[1:]:
        gain = gain * one(*cut)
    return gain


def noise(key, shape, deviation, reach, cuts=(), held_as=jnp.bfloat16):
    level = steps_of(key, shape, cuts, -0.22, 0.18) if cuts else 1.0
    entries = jax.random.normal(key, shape, jnp.float32) * deviation * level
    return jnp.minimum(jnp.maximum(entries, -reach), reach).astype(held_as)


def heavy_noise(own_key, dims, scale, limit, cuts, heavy, kind=jnp.bfloat16):
    entries = scale * jax.random.normal(own_key, dims, jnp.float32)
    if cuts:
        entries = entries * steps_of(own_key, dims, cuts, -0.22, 0.18)
    return jnp.clip(spiked(entries, jax.random.fold_in(own_key, 3), *heavy), -limit, limit).astype(kind)


def setup_inputs(seed: int = 0) -> dict:
    streams_of = jax.random.split(jax.random.key(seed), 12)
    return {
        "tokens": draw_tokens(jax.random.fold_in(streams_of[11], 71), 0),
        "norm_gain": jnp.clip(1.0 + 0.1 * jax.random.normal(streams_of[1], (D,), jnp.float32), 0.5, 1.5),
        "eraser_mean": noise(streams_of[2], (D,), 1.0, 6.0, ((0, 4),), jnp.float32),
        "eraser_in": noise(streams_of[3], (D, K), D ** -0.5, 0.09375, ((0, 4),), jnp.float32),
        "eraser_out": noise(streams_of[4], (D, K), K ** -0.5, 0.5, ((0, 4),), jnp.float32),
        "router": noise(streams_of[5], (D, E), D ** -0.5, 0.09375, ((0, 4),), jnp.float32),
        "expert_ids": draw_expert_ids(jax.random.fold_in(streams_of[11], 71), 0),
        "slots": draw_slots(jax.random.fold_in(streams_of[11], 71), 0),
        "w_gate": noise(streams_of[8], (E * FF_PARTS, D, FF // FF_PARTS), D ** -0.5, 0.09375, ((0, 8), (2, 4))),
        "w_up": noise(streams_of[9], (E * FF_PARTS, D, FF // FF_PARTS), D ** -0.5, 0.09375, ((0, 8), (2, 4))),
        "w_down": heavy_noise(streams_of[10], (E * FF_PARTS, FF // FF_PARTS, D), FF ** -0.5, 0.0625, ((0, 8), (1, 4)), (1, 2, 4, 2.0)),
    }


def reference(tokens, norm_gain, eraser_mean, eraser_in, eraser_out, router, expert_ids, slots, w_gate, w_up, w_down):
    highest = lax.Precision.HIGHEST
    values = tokens.astype(jnp.float32)
    inv_rms = lax.rsqrt(lax.optimization_barrier(jnp.mean(values * values, axis=1, keepdims=True)) + 1e-05)
    normed = values * norm_gain[None, :] * inv_rms
    projected = jnp.dot(normed - eraser_mean[None, :], eraser_in, precision=highest, preferred_element_type=jnp.float32)
    cleaned = normed - jnp.dot(projected, eraser_out.T, precision=highest, preferred_element_type=jnp.float32)
    erased = cleaned.astype(jnp.bfloat16)
    logits = jnp.dot(cleaned, router, precision=highest, preferred_element_type=jnp.float32)
    chosen = (expert_ids[:, :, None] == jnp.arange(E, dtype=jnp.int32)[None, None, :]).astype(jnp.float32)
    picked = lax.optimization_barrier(jnp.sum(chosen * logits[:, None, :], axis=2))
    first_gate = jax.nn.sigmoid(picked[:, 0] - picked[:, 1])
    gate_pair = jnp.stack([first_gate, 1.0 - first_gate], axis=1)
    kept_mask = slots < CAP
    blocks = TOKENS // TOK_DEV
    block_index = (jnp.arange(TOKENS, dtype=jnp.int32) // TOK_DEV).astype(jnp.int32)
    target = block_index[:, None] * CAP + slots
    columns = jnp.arange(blocks * CAP, dtype=jnp.int32)
    erased_wide = erased.astype(jnp.float32)
    combined = jnp.zeros((TOKENS, D), jnp.float32)
    for expert in range(E):
        match = ((target[:, :, None] == columns[None, None, :]) & ((expert_ids == expert) & kept_mask)[:, :, None]).astype(jnp.float32)
        placing = lax.optimization_barrier(jnp.sum(match, axis=1))
        weights = lax.optimization_barrier(jnp.sum(match * gate_pair[:, :, None], axis=1))
        buffer = jnp.dot(placing.T, erased_wide, precision=highest, preferred_element_type=jnp.float32)
        outputs = jnp.zeros((blocks * CAP, D), jnp.float32)
        for piece in range(FF_PARTS):
            index = expert * FF_PARTS + piece
            gate_act = jnp.dot(buffer, w_gate[index].astype(jnp.float32), precision=highest, preferred_element_type=jnp.float32)
            up_act = jnp.dot(buffer, w_up[index].astype(jnp.float32), precision=highest, preferred_element_type=jnp.float32)
            hidden = (jax.nn.silu(gate_act) * up_act).astype(jnp.bfloat16)
            outputs = outputs + jnp.dot(hidden.astype(jnp.float32), w_down[index].astype(jnp.float32), precision=highest, preferred_element_type=jnp.float32)
        combined = combined + jnp.dot(weights, outputs, precision=highest, preferred_element_type=jnp.float32)
    return combined.astype(jnp.bfloat16)
```

```python
import jax
import jax.numpy as jnp
from jax import lax
from jax.sharding import PartitionSpec as P

E = 8


def on_device(
    tokens,
    norm_gain,
    eraser_mean,
    eraser_in,
    eraser_out,
    router,
    expert_ids,
    slots,
    w_gate,
    w_up,
    w_down,
):
    highest = lax.Precision.HIGHEST
    part_count = lax.axis_size("dp") // E
    tok_rows = tokens.shape[0]
    capacity = 3 * tok_rows // 8
    width = tokens.shape[1] * lax.axis_size("tensor")
    values = tokens.astype(jnp.float32)
    gained = values * norm_gain[None, :]
    squares = jnp.sum(values * values, axis=1)
    gained_in = jnp.dot(gained, eraser_in, precision=highest, preferred_element_type=jnp.float32)
    mean_in = jnp.dot(
        eraser_mean[None, :], eraser_in, precision=highest, preferred_element_type=jnp.float32
    )
    router_out = jnp.dot(
        router.T, eraser_out, precision=highest, preferred_element_type=jnp.float32
    )
    routed = jnp.dot(
        router.T, gained.T, precision=highest, preferred_element_type=jnp.float32
    )
    rank = eraser_in.shape[1]
    narrow = jnp.concatenate([routed, squares[None, :]], axis=0)
    narrow = jnp.pad(narrow, ((0, 0), (0, rank - tok_rows)))
    packed = lax.psum(
        jnp.concatenate([gained_in, router_out, mean_in, narrow], axis=0), "tensor"
    )
    gained_in = packed[:tok_rows]
    router_out = packed[tok_rows : tok_rows + E]
    mean_in = packed[tok_rows + E]
    routed = packed[tok_rows + E + 1 : tok_rows + 2 * E + 1, :tok_rows].T
    squares = packed[tok_rows + 2 * E + 1, :tok_rows]
    inv_rms = lax.rsqrt(squares / width + 1e-05)
    projected = inv_rms[:, None] * gained_in - mean_in[None, :]
    cleaned = inv_rms[:, None] * gained - jnp.dot(
        projected, eraser_out.T, precision=highest, preferred_element_type=jnp.float32
    )
    logits = inv_rms[:, None] * routed - jnp.dot(
        projected, router_out.T, precision=highest, preferred_element_type=jnp.float32
    )
    erased = cleaned.astype(jnp.bfloat16)
    chosen = (expert_ids[:, :, None] == jnp.arange(E, dtype=jnp.int32)[None, None, :]).astype(
        jnp.float32
    )
    picked = jnp.sum(chosen * logits[:, None, :], axis=2)
    first_gate = jax.nn.sigmoid(picked[:, 0] - picked[:, 1])
    gate_pair = jnp.stack([first_gate, 1.0 - first_gate], axis=1)
    kept_mask = slots < capacity
    target = expert_ids * capacity + slots
    columns = jnp.arange(E * capacity, dtype=jnp.int32)
    match = ((target[:, :, None] == columns[None, None, :]) & kept_mask[:, :, None]).astype(
        jnp.float32
    )
    placing = jnp.sum(match, axis=1).T.astype(jnp.bfloat16)
    weights = jnp.sum(match * gate_pair[:, :, None], axis=1)
    filled = jnp.dot(placing, erased, preferred_element_type=jnp.float32).astype(jnp.bfloat16)
    received = lax.all_to_all(
        jnp.repeat(filled.reshape(E, capacity, erased.shape[1]), part_count, axis=0),
        "dp",
        split_axis=0,
        concat_axis=0,
        tiled=True,
    )
    received = lax.all_gather(received, "tensor", axis=2, tiled=True)
    sources, count, features = received.shape
    flat_rows = received.reshape(sources * count, features)
    gate_act = jnp.dot(flat_rows, w_gate[0], preferred_element_type=jnp.float32)
    up_act = jnp.dot(flat_rows, w_up[0], preferred_element_type=jnp.float32)
    hidden = (jax.nn.silu(gate_act) * up_act).astype(jnp.bfloat16)
    outputs = jnp.dot(hidden, w_down[0], preferred_element_type=jnp.float32).reshape(
        sources, count, features
    ).astype(jnp.bfloat16)
    reduced = lax.psum_scatter(outputs, "tensor", scatter_dimension=2, tiled=True)
    returned = lax.all_to_all(reduced, "dp", split_axis=0, concat_axis=0, tiled=True)
    summed = jnp.sum(returned.astype(jnp.float32).reshape(E, part_count, capacity, returned.shape[2]), axis=1).reshape(
        E * capacity, returned.shape[2]
    )
    mixed = jnp.dot(weights, summed, precision=highest, preferred_element_type=jnp.float32)
    return mixed.astype(jnp.bfloat16)


def solution(mesh):
    in_specs = (
        P("dp", "tensor"),
        P("tensor"),
        P("tensor"),
        P("tensor", None),
        P("tensor", None),
        P("tensor", None),
        P("dp", None),
        P("dp", None),
        P("dp", None, "tensor"),
        P("dp", None, "tensor"),
        P("dp", "tensor", None),
    )
    out_specs = P("dp", "tensor")
    return jax.shard_map(
        on_device, mesh=mesh, in_specs=in_specs, out_specs=out_specs, check_vma=False
    )
```

```python
import functools

import jax
import jax.numpy as jnp
from jax import lax
from jax.experimental import pallas as pl
from jax.experimental.pallas import tpu as pltpu
from jax.sharding import PartitionSpec as P

E = 8
HIGHEST = lax.Precision.HIGHEST
MESH = pl.DeviceIdType.MESH


def layer_kernel(
    n,
    tensors,
    tok_rows,
    capacity,
    chunk,
    span,
    packed,
    gained,
    eraser_out,
    placing,
    w_gate,
    w_up,
    w_down,
    ret,
    stats,
    stat_in,
    filled,
    xbuf,
    xall,
    hidden,
    gbuf,
    ubuf,
    dbuf,
    part_out,
    part_in,
    pair_out,
    pair_in,
    ret_out,
    gate_sem,
    up_sem,
    down_sem,
    stat_send,
    stat_recv,
    a2a_send,
    a2a_recv,
    near_send,
    near_recv,
    far_send,
    far_recv,
    fwd_send,
    fwd_recv,
    part_send,
    part_recv,
    pair_send,
    pair_recv,
    ret_send,
    ret_recv,
):
    dp = lax.axis_index("dp")
    me = lax.axis_index("tensor")
    side = lax.rem(me, 2)
    row = me // 2
    rows_y = tensors // 2
    partner = row * 2 + (1 - side)
    part_count = n // E
    width = gained.shape[1]
    pieces = width // span
    ff_local = w_gate.shape[2]
    gate_chunks = ff_local // chunk
    gate_slots = gbuf.shape[0]
    down_slots = dbuf.shape[0]
    down_chunks = tensors * pieces

    def gate_copy(c):
        slot = lax.rem(c, gate_slots)
        cols = pl.ds(pl.multiple_of(c * chunk, chunk), chunk)
        return (
            pltpu.make_async_copy(w_gate.at[0, :, cols], gbuf.at[slot], gate_sem.at[slot]),
            pltpu.make_async_copy(w_up.at[0, :, cols], ubuf.at[slot], up_sem.at[slot]),
        )

    def down_owner(i):
        g = i // pieces
        far = g < 2 * (rows_y - 1)
        there = lax.rem(row + 1 + g // 2, rows_y)
        return jnp.where(far, there, row) * 2 + jnp.where(
            lax.rem(g, 2) == 0, 1 - side, side
        )

    def down_copy(i):
        slot = lax.rem(i, down_slots)
        start = down_owner(i) * width + lax.rem(i, pieces) * span
        cols = pl.ds(pl.multiple_of(start, span), span)
        return pltpu.make_async_copy(w_down.at[0, :, cols], dbuf.at[slot], down_sem.at[slot])

    def remote(src, dst, send, recv, device):
        return pltpu.make_async_remote_copy(
            src_ref=src,
            dst_ref=dst,
            send_sem=send,
            recv_sem=recv,
            device_id=device,
            device_id_type=MESH,
        )

    def in_row(t):
        return (dp, t)

    def in_column(d):
        return (d, me)

    @pl.loop(0, gate_slots)
    def _(c):
        one, two = gate_copy(c)
        one.start()
        two.start()

    @pl.loop(0, down_slots)
    def _(i):
        down_copy(i).start()

    barrier = pltpu.get_barrier_semaphore()
    for j in range(1, tensors):
        pl.semaphore_signal(
            barrier, inc=1, device_id=in_row(lax.rem(me + j, tensors)), device_id_type=MESH
        )
    for d in range(1, n):
        pl.semaphore_signal(
            barrier, inc=1, device_id=in_column(lax.rem(dp + d, n)), device_id_type=MESH
        )
    pl.semaphore_wait(barrier, tensors - 1 + n - 1)

    stat_copies = [
        remote(
            packed,
            stat_in.at[j - 1],
            stat_send.at[j - 1],
            stat_recv.at[j - 1],
            in_row(lax.rem(me + j, tensors)),
        )
        for j in range(1, tensors)
    ]
    for copy in stat_copies:
        copy.start()
    for copy in stat_copies:
        copy.wait()
    total = packed[...]
    for j in range(tensors - 1):
        total = total + stat_in[j]
    stats[...] = total

    mean_row = tok_rows + 2 * E
    inv = lax.rsqrt(
        stats[mean_row + 1 : mean_row + 2, :tok_rows] / (width * tensors) + 1e-05
    )
    down_index = lax.broadcasted_iota(jnp.int32, (tok_rows, tok_rows), 0)
    over_index = lax.broadcasted_iota(jnp.int32, (tok_rows, tok_rows), 1)
    inv_rms = jnp.sum(
        jnp.where(down_index == over_index, jnp.broadcast_to(inv, (tok_rows, tok_rows)), 0.0),
        axis=1,
        keepdims=True,
    )
    projected = inv_rms * stats[:tok_rows, :] - stats[mean_row : mean_row + 1, :]
    cleaned = inv_rms * gained[...] - lax.dot_general(
        projected,
        eraser_out[...],
        (((1,), (1,)), ((), ())),
        precision=HIGHEST,
        preferred_element_type=jnp.float32,
    )
    erased = cleaned.astype(jnp.bfloat16)
    placed = jnp.dot(placing[...], erased, preferred_element_type=jnp.float32)
    for e in range(E):
        filled[e] = placed[e * capacity : (e + 1) * capacity].astype(jnp.bfloat16)

    a2a = []
    for d in range(1, n):
        to = lax.rem(dp + d, n)
        a2a.append(
            remote(
                filled.at[to // part_count],
                xbuf.at[me, d],
                a2a_send.at[d - 1],
                a2a_recv.at[d - 1],
                in_column(to),
            )
        )
    for copy in a2a:
        copy.start()
    xbuf[me, 0] = filled[dp // part_count]

    near, far, forward = [], [], []
    lag = 2
    for d in range(n + lag):
        if d < n:
            if d > 0:
                a2a[d - 1].wait_recv()
            for j in range(1, rows_y):
                copy = remote(
                    xbuf.at[me, d],
                    xbuf.at[me, d],
                    far_send.at[j - 1, d],
                    far_recv.at[j - 1, d],
                    in_row(lax.rem(row + j, rows_y) * 2 + side),
                )
                copy.start()
                far.append(copy)
            copy = remote(
                xbuf.at[me, d],
                xbuf.at[me, d],
                near_send.at[d],
                near_recv.at[d],
                in_row(partner),
            )
            copy.start()
            near.append(copy)
        if d >= lag:
            b = d - lag
            for j in range(1, rows_y):
                source = lax.rem(row - j + rows_y, rows_y) * 2 + side
                far[b * (rows_y - 1) + j - 1].wait_recv()
                copy = remote(
                    xbuf.at[source, b],
                    xbuf.at[source, b],
                    fwd_send.at[j - 1, b],
                    fwd_recv.at[j - 1, b],
                    in_row(partner),
                )
                copy.start()
                forward.append(copy)
    for copy in near:
        copy.wait_recv()
    for copy in forward:
        copy.wait_recv()

    for t in range(tensors):
        block = xbuf[t].astype(jnp.float32).reshape(n * capacity, width)
        xall[:, t * width : (t + 1) * width] = block.astype(jnp.bfloat16)

    @pl.loop(0, gate_chunks)
    def _(c):
        slot = lax.rem(c, gate_slots)
        one, two = gate_copy(c)
        one.wait()
        gate = jnp.dot(xall[...], gbuf[slot], preferred_element_type=jnp.float32)
        two.wait()
        up = jnp.dot(xall[...], ubuf[slot], preferred_element_type=jnp.float32)
        cols = pl.ds(pl.multiple_of(c * chunk, chunk), chunk)
        hidden[:, cols] = (gate / (1.0 + jnp.exp(-gate)) * up).astype(jnp.bfloat16)

        @pl.when(c + gate_slots < gate_chunks)
        def _():
            first, second = gate_copy(c + gate_slots)
            first.start()
            second.start()

    def down(i):
        slot = lax.rem(i, down_slots)
        down_copy(i).wait()
        result = jnp.dot(hidden[...], dbuf[slot], preferred_element_type=jnp.float32)

        @pl.when(i + down_slots < down_chunks)
        def _():
            down_copy(i + down_slots).start()

        return result

    def part_copy(j, s):
        return remote(
            part_out.at[j, s],
            part_in.at[j, s],
            part_send.at[j, s],
            part_recv.at[j, s],
            in_row(partner),
        )

    def pair_copy(j, s):
        return remote(
            pair_out.at[j, s],
            pair_in.at[j, s],
            pair_send.at[j, s],
            pair_recv.at[j, s],
            in_row(lax.rem(row + 1 + j, rows_y) * 2 + side),
        )

    def ret_copy(d, s):
        return remote(
            ret_out.at[s, d],
            ret.at[dp, s],
            ret_send.at[d - 1, s],
            ret_recv.at[d - 1, s],
            in_column(lax.rem(dp - d + n, n)),
        )

    for j in range(rows_y):

        @pl.loop(0, pieces)
        def _(s, j=j):
            part_out[j, s] = down(2 * j * pieces + s).astype(jnp.bfloat16)
            part_copy(j, s).start()

        if j < rows_y - 1:

            @pl.loop(0, pieces)
            def _(s, j=j):
                mine = down((2 * j + 1) * pieces + s)
                part_copy(j, s).wait_recv()
                pair_out[j, s] = (mine + part_in[j, s].astype(jnp.float32)).astype(jnp.bfloat16)
                pair_copy(j, s).start()

    last = rows_y - 1

    @pl.loop(0, pieces)
    def _(s):
        mine = down((2 * last + 1) * pieces + s)
        part_copy(last, s).wait_recv()
        mine = mine + part_in[last, s].astype(jnp.float32)
        for j in range(last):
            pair_copy(j, s).wait_recv()
            mine = mine + pair_in[j, s].astype(jnp.float32)
        for d in range(n):
            ret_out[s, d] = mine[d * capacity : (d + 1) * capacity].astype(jnp.bfloat16)
        for d in range(1, n):
            ret_copy(d, s).start()
        ret[dp, s] = ret_out[s, 0]

    for copy in a2a:
        copy.wait_send()
    for copy in near + far + forward:
        copy.wait_send()

    @pl.loop(0, pieces)
    def _(s):
        for j in range(rows_y):
            part_copy(j, s).wait_send()
        for j in range(last):
            pair_copy(j, s).wait_send()
        for d in range(1, n):
            ret_copy(d, s).wait_send()
            ret_copy(d, s).wait_recv()


def on_device(
    tokens,
    norm_gain,
    eraser_mean,
    eraser_in,
    eraser_out,
    router,
    expert_ids,
    slots,
    w_gate,
    w_up,
    w_down,
):
    n = lax.axis_size("dp")
    tensors = lax.axis_size("tensor")
    part_count = n // E
    tok_rows, width = tokens.shape
    capacity = 3 * tok_rows // 8
    rank = eraser_in.shape[1]
    values = tokens.astype(jnp.float32)
    gained = values * norm_gain[None, :]
    squares = jnp.sum(values * values, axis=1)
    gained_in = jnp.dot(gained, eraser_in, precision=HIGHEST, preferred_element_type=jnp.float32)
    mean_in = jnp.dot(
        eraser_mean[None, :], eraser_in, precision=HIGHEST, preferred_element_type=jnp.float32
    )
    router_out = jnp.dot(
        router.T, eraser_out, precision=HIGHEST, preferred_element_type=jnp.float32
    )
    routed = jnp.dot(router.T, gained.T, precision=HIGHEST, preferred_element_type=jnp.float32)
    side_pad = ((0, 0), (0, rank - tok_rows))
    packed = jnp.concatenate(
        [
            gained_in,
            router_out,
            jnp.pad(routed, side_pad),
            mean_in,
            jnp.pad(squares[None, :], side_pad),
            jnp.zeros((6, rank), jnp.float32),
        ],
        axis=0,
    )
    kept_mask = slots < capacity
    target = expert_ids * capacity + slots
    columns = jnp.arange(E * capacity, dtype=jnp.int32)
    match = ((target[:, :, None] == columns[None, None, :]) & kept_mask[:, :, None]).astype(
        jnp.float32
    )
    placing = jnp.sum(match, axis=1).T.astype(jnp.bfloat16)

    hidden_local = w_gate.shape[2]
    chunk = 256 if hidden_local % 256 == 0 else 128
    span = 256
    pieces = width // span
    rows_y = tensors // 2
    rows = n * capacity
    full = width * tensors
    gate_slots = min(6, hidden_local // chunk)
    down_slots = min(8, tensors * pieces)
    bf16 = jnp.bfloat16
    dma = pltpu.SemaphoreType.DMA
    vmem = pl.BlockSpec(memory_space=pltpu.VMEM)
    hbm = pl.BlockSpec(memory_space=pl.ANY)
    ret, stats = pl.pallas_call(
        functools.partial(layer_kernel, n, tensors, tok_rows, capacity, chunk, span),
        out_shape=(
            jax.ShapeDtypeStruct((n, pieces, capacity, span), bf16),
            jax.ShapeDtypeStruct(packed.shape, jnp.float32),
        ),
        in_specs=[vmem] * 4 + [hbm] * 3,
        out_specs=(vmem, vmem),
        scratch_shapes=[
            pltpu.VMEM((tensors - 1,) + packed.shape, jnp.float32),
            pltpu.VMEM((E, capacity, width), bf16),
            pltpu.VMEM((tensors, n, capacity, width), bf16),
            pltpu.VMEM((rows, full), bf16),
            pltpu.VMEM((rows, hidden_local), bf16),
            pltpu.VMEM((gate_slots, full, chunk), bf16),
            pltpu.VMEM((gate_slots, full, chunk), bf16),
            pltpu.VMEM((down_slots, hidden_local, span), bf16),
            pltpu.VMEM((rows_y, pieces, rows, span), bf16),
            pltpu.VMEM((rows_y, pieces, rows, span), bf16),
            pltpu.VMEM((rows_y - 1, pieces, rows, span), bf16),
            pltpu.VMEM((rows_y - 1, pieces, rows, span), bf16),
            pltpu.VMEM((pieces, n, capacity, span), bf16),
            dma((gate_slots,)),
            dma((gate_slots,)),
            dma((down_slots,)),
            dma((tensors - 1,)),
            dma((tensors - 1,)),
            dma((n - 1,)),
            dma((n - 1,)),
            dma((n,)),
            dma((n,)),
            dma((rows_y - 1, n)),
            dma((rows_y - 1, n)),
            dma((rows_y - 1, n)),
            dma((rows_y - 1, n)),
            dma((rows_y, pieces)),
            dma((rows_y, pieces)),
            dma((rows_y - 1, pieces)),
            dma((rows_y - 1, pieces)),
            dma((n - 1, pieces)),
            dma((n - 1, pieces)),
        ],
        compiler_params=pltpu.CompilerParams(
            collective_id=0, has_side_effects=True, vmem_limit_bytes=67043328
        ),
        name="layer",
    )(packed, gained, eraser_out, placing, w_gate, w_up, w_down)

    gained_in = stats[:tok_rows]
    router_out = stats[tok_rows : tok_rows + E]
    routed = stats[tok_rows + E : tok_rows + 2 * E, :tok_rows].T
    mean_in = stats[tok_rows + 2 * E]
    squares = stats[tok_rows + 2 * E + 1, :tok_rows]
    inv_rms = lax.rsqrt(squares / full + 1e-05)
    projected = inv_rms[:, None] * gained_in - mean_in[None, :]
    logits = inv_rms[:, None] * routed - jnp.dot(
        projected, router_out.T, precision=HIGHEST, preferred_element_type=jnp.float32
    )
    chosen = (expert_ids[:, :, None] == jnp.arange(E, dtype=jnp.int32)[None, None, :]).astype(
        jnp.float32
    )
    picked = jnp.sum(chosen * logits[:, None, :], axis=2)
    first_gate = jax.nn.sigmoid(picked[:, 0] - picked[:, 1])
    gate_pair = jnp.stack([first_gate, 1.0 - first_gate], axis=1)
    weights = jnp.sum(match * gate_pair[:, :, None], axis=1)
    summed = jnp.sum(
        ret.astype(jnp.float32).reshape(E, part_count, pieces, capacity, span), axis=1
    )
    summed = summed.transpose(0, 2, 1, 3).reshape(E * capacity, width)
    mixed = jnp.dot(weights, summed, precision=HIGHEST, preferred_element_type=jnp.float32)
    return mixed.astype(jnp.bfloat16)


def solution(mesh):
    in_specs = (
        P("dp", "tensor"),
        P("tensor"),
        P("tensor"),
        P("tensor", None),
        P("tensor", None),
        P("tensor", None),
        P("dp", None),
        P("dp", None),
        P("dp", None, "tensor"),
        P("dp", None, "tensor"),
        P("dp", "tensor", None),
    )
    out_specs = P("dp", "tensor")
    return jax.shard_map(
        on_device, mesh=mesh, in_specs=in_specs, out_specs=out_specs, check_vma=False
    )
```

```python
import functools

import jax
import jax.numpy as jnp
from jax import lax
from jax.experimental import pallas as pl
from jax.experimental.pallas import tpu as pltpu
from jax.sharding import PartitionSpec as P

E = 8
HIGHEST = lax.Precision.HIGHEST
MESH = pl.DeviceIdType.MESH


def layer_kernel(
    n,
    tensors,
    tok_rows,
    capacity,
    chunk,
    span,
    tokens,
    norm_gain,
    eraser_mean,
    eraser_in,
    eraser_out,
    router_t,
    expert_ids,
    slots,
    w_gate,
    w_up,
    w_down,
    out,
    packed,
    stats,
    weights,
    ret,
    stat_in,
    filled,
    xbuf,
    xall,
    hidden,
    gbuf,
    ubuf,
    dbuf,
    part_out,
    part_in,
    pair_out,
    pair_in,
    ret_out,
    gate_sem,
    up_sem,
    down_sem,
    stat_send,
    stat_recv,
    a2a_send,
    a2a_recv,
    near_send,
    near_recv,
    far_send,
    far_recv,
    fwd_send,
    fwd_recv,
    part_send,
    part_recv,
    pair_send,
    pair_recv,
    ret_send,
    ret_recv,
):
    dp = lax.axis_index("dp")
    me = lax.axis_index("tensor")
    side = lax.rem(me, 2)
    row = me // 2
    rows_y = tensors // 2
    partner = row * 2 + (1 - side)
    part_count = n // E
    width = tokens.shape[1]
    pieces = width // span
    ff_local = w_gate.shape[2]
    gate_chunks = ff_local // chunk
    gate_slots = gbuf.shape[0]
    down_slots = dbuf.shape[0]
    down_chunks = tensors * pieces

    def gate_copy(c):
        slot = lax.rem(c, gate_slots)
        cols = pl.ds(pl.multiple_of(c * chunk, chunk), chunk)
        return (
            pltpu.make_async_copy(w_gate.at[0, :, cols], gbuf.at[slot], gate_sem.at[slot]),
            pltpu.make_async_copy(w_up.at[0, :, cols], ubuf.at[slot], up_sem.at[slot]),
        )

    def down_owner(i):
        g = i // pieces
        far = g < 2 * (rows_y - 1)
        there = lax.rem(row + 1 + g // 2, rows_y)
        return jnp.where(far, there, row) * 2 + jnp.where(
            lax.rem(g, 2) == 0, 1 - side, side
        )

    def down_copy(i):
        slot = lax.rem(i, down_slots)
        start = down_owner(i) * width + lax.rem(i, pieces) * span
        cols = pl.ds(pl.multiple_of(start, span), span)
        return pltpu.make_async_copy(w_down.at[0, :, cols], dbuf.at[slot], down_sem.at[slot])

    def remote(src, dst, send, recv, device):
        return pltpu.make_async_remote_copy(
            src_ref=src,
            dst_ref=dst,
            send_sem=send,
            recv_sem=recv,
            device_id=device,
            device_id_type=MESH,
        )

    def in_row(t):
        return (dp, t)

    def in_column(d):
        return (d, me)

    @pl.loop(0, gate_slots)
    def _(c):
        one, two = gate_copy(c)
        one.start()
        two.start()

    @pl.loop(0, down_slots)
    def _(i):
        down_copy(i).start()

    barrier = pltpu.get_barrier_semaphore()
    for j in range(1, tensors):
        pl.semaphore_signal(
            barrier, inc=1, device_id=in_row(lax.rem(me + j, tensors)), device_id_type=MESH
        )
    for d in range(1, n):
        pl.semaphore_signal(
            barrier, inc=1, device_id=in_column(lax.rem(dp + d, n)), device_id_type=MESH
        )
    down_index = lax.broadcasted_iota(jnp.int32, (tok_rows, tok_rows), 0)
    over_index = lax.broadcasted_iota(jnp.int32, (tok_rows, tok_rows), 1)
    diagonal = down_index == over_index

    def to_row(column):
        wide = jnp.where(diagonal, jnp.broadcast_to(column, (tok_rows, tok_rows)), 0.0)
        return jnp.sum(wide, axis=0, keepdims=True)

    def to_column(line):
        wide = jnp.where(diagonal, jnp.broadcast_to(line, (tok_rows, tok_rows)), 0.0)
        return jnp.sum(wide, axis=1, keepdims=True)

    values = tokens[...].astype(jnp.float32)
    gained = values * norm_gain[...]
    mean_row = tok_rows + 2 * E
    stacked = jnp.concatenate(
        [gained, jnp.broadcast_to(eraser_mean[...], (8, width))], axis=0
    )
    into = jnp.dot(
        stacked, eraser_in[...], precision=HIGHEST, preferred_element_type=jnp.float32
    )
    contract = (((1,), (1,)), ((), ()))
    packed[...] = jnp.zeros_like(packed)
    packed[:tok_rows, :] = into[:tok_rows]
    packed[tok_rows : tok_rows + E, :] = jnp.dot(
        router_t[...], eraser_out[...], precision=HIGHEST, preferred_element_type=jnp.float32
    )
    packed[tok_rows + E : mean_row, :tok_rows] = lax.dot_general(
        router_t[...], gained, contract, precision=HIGHEST, preferred_element_type=jnp.float32
    )
    packed[mean_row : mean_row + 1, :] = into[tok_rows : tok_rows + 1]
    packed[mean_row + 1 : mean_row + 2, :tok_rows] = to_row(
        jnp.sum(values * values, axis=1, keepdims=True)
    )

    choices = []
    for k in range(2):
        expert = expert_ids[k : k + 1, :].astype(jnp.float32)
        slot = slots[k : k + 1, :].astype(jnp.float32)
        choices.append((expert, slot, slot < capacity))
    placing_rows = lax.broadcasted_iota(jnp.int32, (E * capacity, tok_rows), 0).astype(jnp.float32)
    placing = jnp.zeros((E * capacity, tok_rows), jnp.float32)
    for expert, slot, kept in choices:
        target = jnp.where(kept, expert * capacity + slot, -1.0)
        placing = placing + jnp.where(placing_rows == target, 1.0, 0.0)
    placing = placing.astype(jnp.bfloat16)

    pl.semaphore_wait(barrier, tensors - 1 + n - 1)

    stat_copies = [
        remote(
            packed,
            stat_in.at[j - 1],
            stat_send.at[j - 1],
            stat_recv.at[j - 1],
            in_row(lax.rem(me + j, tensors)),
        )
        for j in range(1, tensors)
    ]
    for copy in stat_copies:
        copy.start()
    for copy in stat_copies:
        copy.wait()
    total = packed[...]
    for j in range(tensors - 1):
        total = total + stat_in[j]
    stats[...] = total

    inv = lax.rsqrt(
        stats[mean_row + 1 : mean_row + 2, :tok_rows] / (width * tensors) + 1e-05
    )
    inv_rms = to_column(inv)
    projected = inv_rms * stats[:tok_rows, :] - stats[mean_row : mean_row + 1, :]
    cleaned = inv_rms * gained - lax.dot_general(
        projected,
        eraser_out[...],
        contract,
        precision=HIGHEST,
        preferred_element_type=jnp.float32,
    )
    erased = cleaned.astype(jnp.bfloat16)
    placed = jnp.dot(placing, erased, preferred_element_type=jnp.float32)
    for e in range(E):
        filled[e] = placed[e * capacity : (e + 1) * capacity].astype(jnp.bfloat16)

    a2a = []
    for d in range(1, n):
        to = lax.rem(dp + d, n)
        a2a.append(
            remote(
                filled.at[to // part_count],
                xbuf.at[me, d],
                a2a_send.at[d - 1],
                a2a_recv.at[d - 1],
                in_column(to),
            )
        )
    for copy in a2a:
        copy.start()
    xbuf[me, 0] = filled[dp // part_count]

    logits = inv * stats[tok_rows + E : mean_row, :tok_rows] - lax.dot_general(
        stats[tok_rows : tok_rows + E, :],
        projected,
        contract,
        precision=HIGHEST,
        preferred_element_type=jnp.float32,
    )
    expert_rows = lax.broadcasted_iota(jnp.int32, (E, tok_rows), 0).astype(jnp.float32)
    picked = [
        jnp.sum(
            jnp.where(expert_rows == expert, logits, 0.0),
            axis=0,
            keepdims=True,
        )
        for expert, slot, kept in choices
    ]
    first_gate = to_column(1.0 / (1.0 + jnp.exp(picked[1] - picked[0])))
    slot_columns = lax.broadcasted_iota(jnp.int32, (tok_rows, n * capacity), 1)
    slot_columns = slot_columns.astype(jnp.float32)
    mix = jnp.zeros((tok_rows, n * capacity), jnp.float32)
    for (expert, slot, kept), gate in zip(choices, (first_gate, 1.0 - first_gate)):
        for part in range(part_count):
            target = jnp.where(kept, (expert * part_count + part) * capacity + slot, -1.0)
            mix = mix + jnp.where(slot_columns == to_column(target), gate, 0.0)
    high = mix.astype(jnp.bfloat16)
    rest = mix - high.astype(jnp.float32)
    middle = rest.astype(jnp.bfloat16)
    low = (rest - middle.astype(jnp.float32)).astype(jnp.bfloat16)
    weights[0] = high
    weights[1] = middle
    weights[2] = low

    near, far, forward = [], [], []
    lag = 2
    for d in range(n + lag):
        if d < n:
            if d > 0:
                a2a[d - 1].wait_recv()
            for j in range(1, rows_y):
                copy = remote(
                    xbuf.at[me, d],
                    xbuf.at[me, d],
                    far_send.at[j - 1, d],
                    far_recv.at[j - 1, d],
                    in_row(lax.rem(row + j, rows_y) * 2 + side),
                )
                copy.start()
                far.append(copy)
            copy = remote(
                xbuf.at[me, d],
                xbuf.at[me, d],
                near_send.at[d],
                near_recv.at[d],
                in_row(partner),
            )
            copy.start()
            near.append(copy)
        if d >= lag:
            b = d - lag
            for j in range(1, rows_y):
                source = lax.rem(row - j + rows_y, rows_y) * 2 + side
                far[b * (rows_y - 1) + j - 1].wait_recv()
                copy = remote(
                    xbuf.at[source, b],
                    xbuf.at[source, b],
                    fwd_send.at[j - 1, b],
                    fwd_recv.at[j - 1, b],
                    in_row(partner),
                )
                copy.start()
                forward.append(copy)
    for copy in near:
        copy.wait_recv()
    for copy in forward:
        copy.wait_recv()

    for t in range(tensors):
        block = xbuf[t].astype(jnp.float32).reshape(n * capacity, width)
        xall[:, t * width : (t + 1) * width] = block.astype(jnp.bfloat16)

    @pl.loop(0, gate_chunks)
    def _(c):
        slot = lax.rem(c, gate_slots)
        one, two = gate_copy(c)
        one.wait()
        gate = jnp.dot(xall[...], gbuf[slot], preferred_element_type=jnp.float32)
        two.wait()
        up = jnp.dot(xall[...], ubuf[slot], preferred_element_type=jnp.float32)
        cols = pl.ds(pl.multiple_of(c * chunk, chunk), chunk)
        hidden[:, cols] = (gate / (1.0 + jnp.exp(-gate)) * up).astype(jnp.bfloat16)

        @pl.when(c + gate_slots < gate_chunks)
        def _():
            first, second = gate_copy(c + gate_slots)
            first.start()
            second.start()

    def down(i):
        slot = lax.rem(i, down_slots)
        down_copy(i).wait()
        result = jnp.dot(hidden[...], dbuf[slot], preferred_element_type=jnp.float32)

        @pl.when(i + down_slots < down_chunks)
        def _():
            down_copy(i + down_slots).start()

        return result

    def part_copy(j, s):
        return remote(
            part_out.at[j, s],
            part_in.at[j, s],
            part_send.at[j, s],
            part_recv.at[j, s],
            in_row(partner),
        )

    def pair_copy(j, s):
        return remote(
            pair_out.at[j, s],
            pair_in.at[j, s],
            pair_send.at[j, s],
            pair_recv.at[j, s],
            in_row(lax.rem(row + 1 + j, rows_y) * 2 + side),
        )

    def ret_copy(d, s):
        return remote(
            ret_out.at[s, d],
            ret.at[dp, s],
            ret_send.at[d - 1, s],
            ret_recv.at[d - 1, s],
            in_column(lax.rem(dp - d + n, n)),
        )

    for j in range(rows_y):

        @pl.loop(0, pieces)
        def _(s, j=j):
            part_out[j, s] = down(2 * j * pieces + s).astype(jnp.bfloat16)
            part_copy(j, s).start()

        if j < rows_y - 1:

            @pl.loop(0, pieces)
            def _(s, j=j):
                mine = down((2 * j + 1) * pieces + s)
                part_copy(j, s).wait_recv()
                pair_out[j, s] = (mine + part_in[j, s].astype(jnp.float32)).astype(jnp.bfloat16)
                pair_copy(j, s).start()

    last = rows_y - 1

    @pl.loop(0, pieces)
    def _(s):
        mine = down((2 * last + 1) * pieces + s)
        part_copy(last, s).wait_recv()
        mine = mine + part_in[last, s].astype(jnp.float32)
        for j in range(last):
            pair_copy(j, s).wait_recv()
            mine = mine + pair_in[j, s].astype(jnp.float32)
        for d in range(n):
            ret_out[s, d] = mine[d * capacity : (d + 1) * capacity].astype(jnp.bfloat16)
        for d in range(1, n):
            ret_copy(d, s).start()
        ret[dp, s] = ret_out[s, 0]

    for s in range(pieces):
        for d in range(1, n):
            ret_copy(d, s).wait_recv()
        rows = ret[:, s].astype(jnp.float32).reshape(n * capacity, span).astype(jnp.bfloat16)
        mixed = jnp.dot(weights[2], rows, preferred_element_type=jnp.float32)
        mixed = mixed + jnp.dot(weights[1], rows, preferred_element_type=jnp.float32)
        mixed = mixed + jnp.dot(weights[0], rows, preferred_element_type=jnp.float32)
        out[:, s * span : (s + 1) * span] = mixed.astype(jnp.bfloat16)

    for copy in a2a:
        copy.wait_send()
    for copy in near + far + forward:
        copy.wait_send()

    @pl.loop(0, pieces)
    def _(s):
        for j in range(rows_y):
            part_copy(j, s).wait_send()
        for j in range(last):
            pair_copy(j, s).wait_send()
        for d in range(1, n):
            ret_copy(d, s).wait_send()


def on_device(
    tokens,
    norm_gain,
    eraser_mean,
    eraser_in,
    eraser_out,
    router,
    expert_ids,
    slots,
    w_gate,
    w_up,
    w_down,
):
    n = lax.axis_size("dp")
    tensors = lax.axis_size("tensor")
    tok_rows, width = tokens.shape
    capacity = 3 * tok_rows // 8
    stat_shape = (tok_rows + 2 * E + 8, eraser_in.shape[1])
    hidden_local = w_gate.shape[2]
    chunk = 256 if hidden_local % 256 == 0 else 128
    span = 256
    pieces = width // span
    rows_y = tensors // 2
    rows = n * capacity
    full = width * tensors
    gate_slots = min(8, hidden_local // chunk)
    down_slots = min(8, tensors * pieces)
    bf16 = jnp.bfloat16
    dma = pltpu.SemaphoreType.DMA
    vmem = pl.BlockSpec(memory_space=pltpu.VMEM)
    hbm = pl.BlockSpec(memory_space=pl.ANY)
    return pl.pallas_call(
        functools.partial(layer_kernel, n, tensors, tok_rows, capacity, chunk, span),
        out_shape=jax.ShapeDtypeStruct((tok_rows, width), bf16),
        in_specs=[vmem] * 8 + [hbm] * 3,
        out_specs=vmem,
        scratch_shapes=[
            pltpu.VMEM(stat_shape, jnp.float32),
            pltpu.VMEM(stat_shape, jnp.float32),
            pltpu.VMEM((3, tok_rows, rows), bf16),
            pltpu.VMEM((n, pieces, capacity, span), bf16),
            pltpu.VMEM((tensors - 1,) + stat_shape, jnp.float32),
            pltpu.VMEM((E, capacity, width), bf16),
            pltpu.VMEM((tensors, n, capacity, width), bf16),
            pltpu.VMEM((rows, full), bf16),
            pltpu.VMEM((rows, hidden_local), bf16),
            pltpu.VMEM((gate_slots, full, chunk), bf16),
            pltpu.VMEM((gate_slots, full, chunk), bf16),
            pltpu.VMEM((down_slots, hidden_local, span), bf16),
            pltpu.VMEM((rows_y, pieces, rows, span), bf16),
            pltpu.VMEM((rows_y, pieces, rows, span), bf16),
            pltpu.VMEM((rows_y - 1, pieces, rows, span), bf16),
            pltpu.VMEM((rows_y - 1, pieces, rows, span), bf16),
            pltpu.VMEM((pieces, n, capacity, span), bf16),
            dma((gate_slots,)),
            dma((gate_slots,)),
            dma((down_slots,)),
            dma((tensors - 1,)),
            dma((tensors - 1,)),
            dma((n - 1,)),
            dma((n - 1,)),
            dma((n,)),
            dma((n,)),
            dma((rows_y - 1, n)),
            dma((rows_y - 1, n)),
            dma((rows_y - 1, n)),
            dma((rows_y - 1, n)),
            dma((rows_y, pieces)),
            dma((rows_y, pieces)),
            dma((rows_y - 1, pieces)),
            dma((rows_y - 1, pieces)),
            dma((n - 1, pieces)),
            dma((n - 1, pieces)),
        ],
        compiler_params=pltpu.CompilerParams(
            collective_id=0, has_side_effects=True, vmem_limit_bytes=67043328
        ),
        name="layer",
    )(
        tokens,
        norm_gain[None, :],
        eraser_mean[None, :],
        eraser_in,
        eraser_out,
        router.T,
        expert_ids.T,
        slots.T,
        w_gate,
        w_up,
        w_down,
    )


def solution(mesh):
    in_specs = (
        P("dp", "tensor"),
        P("tensor"),
        P("tensor"),
        P("tensor", None),
        P("tensor", None),
        P("tensor", None),
        P("dp", None),
        P("dp", None),
        P("dp", None, "tensor"),
        P("dp", None, "tensor"),
        P("dp", "tensor", None),
    )
    out_specs = P("dp", "tensor")
    return jax.shard_map(
        on_device, mesh=mesh, in_specs=in_specs, out_specs=out_specs, check_vma=False
    )
```

```python
import functools

import jax
import jax.numpy as jnp
from jax import lax
from jax.experimental import pallas as pl
from jax.experimental.pallas import tpu as pltpu
from jax.sharding import PartitionSpec as P

E = 8
HIGHEST = lax.Precision.HIGHEST
MESH = pl.DeviceIdType.MESH


def layer_kernel(
    n,
    tensors,
    tok_rows,
    capacity,
    chunk,
    span,
    tokens,
    norm_gain,
    eraser_mean,
    eraser_in,
    eraser_out,
    router_t,
    expert_ids,
    slots,
    w_gate,
    w_up,
    w_down,
    out,
    packed,
    stats,
    weights,
    ret,
    stat_in,
    filled,
    xbuf,
    xall,
    hidden,
    gbuf,
    dbuf,
    part_out,
    part_in,
    pair_out,
    pair_in,
    ret_out,
    gate_sem,
    up_sem,
    down_sem,
    stat_send,
    stat_recv,
    a2a_send,
    a2a_recv,
    near_send,
    near_recv,
    far_send,
    far_recv,
    fwd_send,
    fwd_recv,
    part_send,
    part_recv,
    pair_send,
    pair_recv,
    ret_send,
    ret_recv,
):
    dp = lax.axis_index("dp")
    me = lax.axis_index("tensor")
    side = lax.rem(me, 2)
    row = me // 2
    rows_y = tensors // 2
    partner = row * 2 + (1 - side)
    part_count = n // E
    width = tokens.shape[1]
    pieces = width // span
    ff_local = w_gate.shape[2]
    gate_chunks = ff_local // chunk
    gate_slots = gbuf.shape[0]
    down_slots = dbuf.shape[0]
    down_chunks = tensors * pieces

    def gate_copy(c):
        slot = lax.rem(c, gate_slots)
        cols = pl.ds(pl.multiple_of(c * chunk, chunk), chunk)
        return (
            pltpu.make_async_copy(w_gate.at[0, :, cols], gbuf.at[slot, :, :chunk], gate_sem.at[slot]),
            pltpu.make_async_copy(w_up.at[0, :, cols], gbuf.at[slot, :, chunk:], up_sem.at[slot]),
        )

    def down_owner(i):
        g = i // pieces
        far = g < 2 * (rows_y - 1)
        there = lax.rem(row + 1 + g // 2, rows_y)
        return jnp.where(far, there, row) * 2 + jnp.where(
            lax.rem(g, 2) == 0, 1 - side, side
        )

    def down_copy(i):
        slot = lax.rem(i, down_slots)
        start = down_owner(i) * width + lax.rem(i, pieces) * span
        cols = pl.ds(pl.multiple_of(start, span), span)
        return pltpu.make_async_copy(w_down.at[0, :, cols], dbuf.at[slot], down_sem.at[slot])

    def remote(src, dst, send, recv, device):
        return pltpu.make_async_remote_copy(
            src_ref=src,
            dst_ref=dst,
            send_sem=send,
            recv_sem=recv,
            device_id=device,
            device_id_type=MESH,
        )

    def in_row(t):
        return (dp, t)

    def in_column(d):
        return (d, me)

    @pl.loop(0, gate_slots)
    def _(c):
        one, two = gate_copy(c)
        one.start()
        two.start()

    @pl.loop(0, down_slots)
    def _(i):
        down_copy(i).start()

    barrier = pltpu.get_barrier_semaphore()
    for j in range(1, tensors):
        pl.semaphore_signal(
            barrier, inc=1, device_id=in_row(lax.rem(me + j, tensors)), device_id_type=MESH
        )
    for d in range(1, n):
        pl.semaphore_signal(
            barrier, inc=1, device_id=in_column(lax.rem(dp + d, n)), device_id_type=MESH
        )
    down_index = lax.broadcasted_iota(jnp.int32, (tok_rows, tok_rows), 0)
    over_index = lax.broadcasted_iota(jnp.int32, (tok_rows, tok_rows), 1)
    diagonal = down_index == over_index

    def to_row(column):
        wide = jnp.where(diagonal, jnp.broadcast_to(column, (tok_rows, tok_rows)), 0.0)
        return jnp.sum(wide, axis=0, keepdims=True)

    def to_column(line):
        wide = jnp.where(diagonal, jnp.broadcast_to(line, (tok_rows, tok_rows)), 0.0)
        return jnp.sum(wide, axis=1, keepdims=True)

    values = tokens[...].astype(jnp.float32)
    gained = values * norm_gain[...]
    mean_row = tok_rows + 2 * E
    stacked = jnp.concatenate(
        [gained, jnp.broadcast_to(eraser_mean[...], (8, width))], axis=0
    )
    into = jnp.dot(
        stacked, eraser_in[...], precision=HIGHEST, preferred_element_type=jnp.float32
    )
    contract = (((1,), (1,)), ((), ()))
    packed[...] = jnp.zeros_like(packed)
    packed[:tok_rows, :] = into[:tok_rows]
    packed[tok_rows : tok_rows + E, :] = jnp.dot(
        router_t[...], eraser_out[...], precision=HIGHEST, preferred_element_type=jnp.float32
    )
    packed[tok_rows + E : mean_row, :tok_rows] = lax.dot_general(
        router_t[...], gained, contract, precision=HIGHEST, preferred_element_type=jnp.float32
    )
    packed[mean_row : mean_row + 1, :] = into[tok_rows : tok_rows + 1]
    packed[mean_row + 1 : mean_row + 2, :tok_rows] = to_row(
        jnp.sum(values * values, axis=1, keepdims=True)
    )

    choices = []
    for k in range(2):
        expert = expert_ids[k : k + 1, :].astype(jnp.float32)
        slot = slots[k : k + 1, :].astype(jnp.float32)
        choices.append((expert, slot, slot < capacity))
    placing_rows = lax.broadcasted_iota(jnp.int32, (E * capacity, tok_rows), 0).astype(jnp.float32)
    placing = jnp.zeros((E * capacity, tok_rows), jnp.float32)
    for expert, slot, kept in choices:
        target = jnp.where(kept, expert * capacity + slot, -1.0)
        placing = placing + jnp.where(placing_rows == target, 1.0, 0.0)
    placing = placing.astype(jnp.bfloat16)

    pl.semaphore_wait(barrier, tensors - 1 + n - 1)

    stat_copies = [
        remote(
            packed,
            stat_in.at[j - 1],
            stat_send.at[j - 1],
            stat_recv.at[j - 1],
            in_row(lax.rem(me + j, tensors)),
        )
        for j in range(1, tensors)
    ]
    for copy in stat_copies:
        copy.start()
    for copy in stat_copies:
        copy.wait()
    total = packed[...]
    for j in range(tensors - 1):
        total = total + stat_in[j]
    stats[...] = total

    inv = lax.rsqrt(
        stats[mean_row + 1 : mean_row + 2, :tok_rows] / (width * tensors) + 1e-05
    )
    inv_rms = to_column(inv)
    projected = inv_rms * stats[:tok_rows, :] - stats[mean_row : mean_row + 1, :]
    cleaned = inv_rms * gained - lax.dot_general(
        projected,
        eraser_out[...],
        contract,
        precision=HIGHEST,
        preferred_element_type=jnp.float32,
    )
    erased = cleaned.astype(jnp.bfloat16)
    placed = jnp.dot(placing, erased, preferred_element_type=jnp.float32)
    for e in range(E):
        filled[e] = placed[e * capacity : (e + 1) * capacity].astype(jnp.bfloat16)

    a2a = []
    for d in range(1, n):
        to = lax.rem(dp + d, n)
        a2a.append(
            remote(
                filled.at[to // part_count],
                xbuf.at[me, d],
                a2a_send.at[d - 1],
                a2a_recv.at[d - 1],
                in_column(to),
            )
        )
    for copy in a2a:
        copy.start()
    xbuf[me, 0] = filled[dp // part_count]

    logits = inv * stats[tok_rows + E : mean_row, :tok_rows] - lax.dot_general(
        stats[tok_rows : tok_rows + E, :],
        projected,
        contract,
        precision=HIGHEST,
        preferred_element_type=jnp.float32,
    )
    expert_rows = lax.broadcasted_iota(jnp.int32, (E, tok_rows), 0).astype(jnp.float32)
    picked = [
        jnp.sum(
            jnp.where(expert_rows == expert, logits, 0.0),
            axis=0,
            keepdims=True,
        )
        for expert, slot, kept in choices
    ]
    first_gate = to_column(1.0 / (1.0 + jnp.exp(picked[1] - picked[0])))
    slot_columns = lax.broadcasted_iota(jnp.int32, (tok_rows, n * capacity), 1)
    slot_columns = slot_columns.astype(jnp.float32)
    mix = jnp.zeros((tok_rows, n * capacity), jnp.float32)
    for (expert, slot, kept), gate in zip(choices, (first_gate, 1.0 - first_gate)):
        for part in range(part_count):
            target = jnp.where(kept, (expert * part_count + part) * capacity + slot, -1.0)
            mix = mix + jnp.where(slot_columns == to_column(target), gate, 0.0)
    high = mix.astype(jnp.bfloat16)
    rest = mix - high.astype(jnp.float32)
    middle = rest.astype(jnp.bfloat16)
    low = (rest - middle.astype(jnp.float32)).astype(jnp.bfloat16)
    weights[0] = high
    weights[1] = middle
    weights[2] = low

    near, far, forward = [], [], []
    lag = 2
    for d in range(n + lag):
        if d < n:
            if d > 0:
                a2a[d - 1].wait_recv()
            for j in range(1, rows_y):
                copy = remote(
                    xbuf.at[me, d],
                    xbuf.at[me, d],
                    far_send.at[j - 1, d],
                    far_recv.at[j - 1, d],
                    in_row(lax.rem(row + j, rows_y) * 2 + side),
                )
                copy.start()
                far.append(copy)
            copy = remote(
                xbuf.at[me, d],
                xbuf.at[me, d],
                near_send.at[d],
                near_recv.at[d],
                in_row(partner),
            )
            copy.start()
            near.append(copy)
        if d >= lag:
            b = d - lag
            for j in range(1, rows_y):
                source = lax.rem(row - j + rows_y, rows_y) * 2 + side
                far[b * (rows_y - 1) + j - 1].wait_recv()
                copy = remote(
                    xbuf.at[source, b],
                    xbuf.at[source, b],
                    fwd_send.at[j - 1, b],
                    fwd_recv.at[j - 1, b],
                    in_row(partner),
                )
                copy.start()
                forward.append(copy)
    for copy in near:
        copy.wait_recv()
    for copy in forward:
        copy.wait_recv()

    for t in range(tensors):
        block = xbuf[t].astype(jnp.float32).reshape(n * capacity, width)
        xall[:, t * width : (t + 1) * width] = block.astype(jnp.bfloat16)

    @pl.loop(0, gate_chunks)
    def _(c):
        slot = lax.rem(c, gate_slots)
        one, two = gate_copy(c)
        one.wait()
        two.wait()
        both = jnp.dot(xall[...], gbuf[slot], preferred_element_type=jnp.float32)
        gate, up = both[:, :chunk], both[:, chunk:]
        cols = pl.ds(pl.multiple_of(c * chunk, chunk), chunk)
        hidden[:, cols] = (gate / (1.0 + jnp.exp(-gate)) * up).astype(jnp.bfloat16)

        @pl.when(c + gate_slots < gate_chunks)
        def _():
            first, second = gate_copy(c + gate_slots)
            first.start()
            second.start()

    def down(i):
        slot = lax.rem(i, down_slots)
        down_copy(i).wait()
        result = jnp.dot(hidden[...], dbuf[slot], preferred_element_type=jnp.float32)

        @pl.when(i + down_slots < down_chunks)
        def _():
            down_copy(i + down_slots).start()

        return result

    def part_copy(j, s):
        return remote(
            part_out.at[j, s],
            part_in.at[j, s],
            part_send.at[j, s],
            part_recv.at[j, s],
            in_row(partner),
        )

    def pair_copy(j, s):
        return remote(
            pair_out.at[j, s],
            pair_in.at[j, s],
            pair_send.at[j, s],
            pair_recv.at[j, s],
            in_row(lax.rem(row + 1 + j, rows_y) * 2 + side),
        )

    def ret_copy(d, s):
        return remote(
            ret_out.at[s, d],
            ret.at[dp, s],
            ret_send.at[d - 1, s],
            ret_recv.at[d - 1, s],
            in_column(lax.rem(dp - d + n, n)),
        )

    for j in range(rows_y):

        @pl.loop(0, pieces)
        def _(s, j=j):
            part_out[j, s] = down(2 * j * pieces + s).astype(jnp.bfloat16)
            part_copy(j, s).start()

        if j < rows_y - 1:

            @pl.loop(0, pieces)
            def _(s, j=j):
                mine = down((2 * j + 1) * pieces + s)
                part_copy(j, s).wait_recv()
                pair_out[j, s] = (mine + part_in[j, s].astype(jnp.float32)).astype(jnp.bfloat16)
                pair_copy(j, s).start()

    last = rows_y - 1

    @pl.loop(0, pieces)
    def _(s):
        mine = down((2 * last + 1) * pieces + s)
        part_copy(last, s).wait_recv()
        mine = mine + part_in[last, s].astype(jnp.float32)
        for j in range(last):
            pair_copy(j, s).wait_recv()
            mine = mine + pair_in[j, s].astype(jnp.float32)
        for d in range(n):
            ret_out[s, d] = mine[d * capacity : (d + 1) * capacity].astype(jnp.bfloat16)
        for d in range(1, n):
            ret_copy(d, s).start()
        ret[dp, s] = ret_out[s, 0]

    for s in range(pieces):
        for d in range(1, n):
            ret_copy(d, s).wait_recv()
        rows = ret[:, s].astype(jnp.float32).reshape(n * capacity, span).astype(jnp.bfloat16)
        mixed = jnp.dot(weights[2], rows, preferred_element_type=jnp.float32)
        mixed = mixed + jnp.dot(weights[1], rows, preferred_element_type=jnp.float32)
        mixed = mixed + jnp.dot(weights[0], rows, preferred_element_type=jnp.float32)
        out[:, s * span : (s + 1) * span] = mixed.astype(jnp.bfloat16)

    for copy in a2a:
        copy.wait_send()
    for copy in near + far + forward:
        copy.wait_send()

    @pl.loop(0, pieces)
    def _(s):
        for j in range(rows_y):
            part_copy(j, s).wait_send()
        for j in range(last):
            pair_copy(j, s).wait_send()
        for d in range(1, n):
            ret_copy(d, s).wait_send()


def on_device(
    tokens,
    norm_gain,
    eraser_mean,
    eraser_in,
    eraser_out,
    router,
    expert_ids,
    slots,
    w_gate,
    w_up,
    w_down,
):
    n = lax.axis_size("dp")
    tensors = lax.axis_size("tensor")
    tok_rows, width = tokens.shape
    capacity = 3 * tok_rows // 8
    stat_shape = (tok_rows + 2 * E + 8, eraser_in.shape[1])
    hidden_local = w_gate.shape[2]
    chunk = 256 if hidden_local % 256 == 0 else 128
    span = min(512, width)
    pieces = width // span
    rows_y = tensors // 2
    rows = n * capacity
    full = width * tensors
    gate_slots = min(7, hidden_local // chunk)
    down_slots = min(4, tensors * pieces)
    bf16 = jnp.bfloat16
    dma = pltpu.SemaphoreType.DMA
    vmem = pl.BlockSpec(memory_space=pltpu.VMEM)
    hbm = pl.BlockSpec(memory_space=pl.ANY)
    return pl.pallas_call(
        functools.partial(layer_kernel, n, tensors, tok_rows, capacity, chunk, span),
        out_shape=jax.ShapeDtypeStruct((tok_rows, width), bf16),
        in_specs=[vmem] * 8 + [hbm] * 3,
        out_specs=vmem,
        scratch_shapes=[
            pltpu.VMEM(stat_shape, jnp.float32),
            pltpu.VMEM(stat_shape, jnp.float32),
            pltpu.VMEM((3, tok_rows, rows), bf16),
            pltpu.VMEM((n, pieces, capacity, span), bf16),
            pltpu.VMEM((tensors - 1,) + stat_shape, jnp.float32),
            pltpu.VMEM((E, capacity, width), bf16),
            pltpu.VMEM((tensors, n, capacity, width), bf16),
            pltpu.VMEM((rows, full), bf16),
            pltpu.VMEM((rows, hidden_local), bf16),
            pltpu.VMEM((gate_slots, full, 2 * chunk), bf16),
            pltpu.VMEM((down_slots, hidden_local, span), bf16),
            pltpu.VMEM((rows_y, pieces, rows, span), bf16),
            pltpu.VMEM((rows_y, pieces, rows, span), bf16),
            pltpu.VMEM((rows_y - 1, pieces, rows, span), bf16),
            pltpu.VMEM((rows_y - 1, pieces, rows, span), bf16),
            pltpu.VMEM((pieces, n, capacity, span), bf16),
            dma((gate_slots,)),
            dma((gate_slots,)),
            dma((down_slots,)),
            dma((tensors - 1,)),
            dma((tensors - 1,)),
            dma((n - 1,)),
            dma((n - 1,)),
            dma((n,)),
            dma((n,)),
            dma((rows_y - 1, n)),
            dma((rows_y - 1, n)),
            dma((rows_y - 1, n)),
            dma((rows_y - 1, n)),
            dma((rows_y, pieces)),
            dma((rows_y, pieces)),
            dma((rows_y - 1, pieces)),
            dma((rows_y - 1, pieces)),
            dma((n - 1, pieces)),
            dma((n - 1, pieces)),
        ],
        compiler_params=pltpu.CompilerParams(
            collective_id=0, has_side_effects=True, vmem_limit_bytes=67043328
        ),
        name="layer",
    )(
        tokens,
        norm_gain[None, :],
        eraser_mean[None, :],
        eraser_in,
        eraser_out,
        router.T,
        expert_ids.T,
        slots.T,
        w_gate,
        w_up,
        w_down,
    )


def solution(mesh):
    in_specs = (
        P("dp", "tensor"),
        P("tensor"),
        P("tensor"),
        P("tensor", None),
        P("tensor", None),
        P("tensor", None),
        P("dp", None),
        P("dp", None),
        P("dp", None, "tensor"),
        P("dp", None, "tensor"),
        P("dp", "tensor", None),
    )
    out_specs = P("dp", "tensor")
    return jax.shard_map(
        on_device, mesh=mesh, in_specs=in_specs, out_specs=out_specs, check_vma=False
    )
```
